32 devices in a mesh: section: 4 (over z), seq: 8 (over y, x, core).
Axes of the slice: x: 2, y: 2, z: 4, core: 2. Of those that a mesh axis runs over, the one named last changes fastest.
Arguments:
- x_a: bfloat16 [1024, 4096], P('seq'), may hold values from -6 to 6
- x_b: bfloat16 [1024, 4096], P('seq'), may hold values from -6 to 6
- grad_a: bfloat16 [1024, 4096], P('seq'), may hold values from -6 to 6
- grad_b: bfloat16 [1024, 4096], P('seq'), may hold values from -6 to 6
- gains: float32 [4, 2, 4096], P('section'), may hold values from 0.5 to 1.5
- kv_weights: bfloat16 [4, 2, 4096, 1024], P('section'), may hold values from -0.09375 to 0.09375
- doc_lengths: int32 [2, 16], replicated, may hold values from 1 to 128, 1024 in all within a row
Outputs:
- acts: bfloat16 [2, 4, 1024, 4096], P(None, 'section', 'seq')
- in_grads: bfloat16 [2, 4, 1024, 4096], P(None, 'section', 'seq')
- kv_grads: bfloat16 [2, 4, 1024, 1024], P(None, 'section', 'seq')
The draws below stay inside these ranges and needn't reach their ends.
Inputs may be any that keep to these rules, and one draw needn't show every extreme that they name: `doc_lengths`: each row lists 16 documents that fill the 1024 tokens of its sequence in order; in each row some document is exactly 128 tokens long.
All inputs are finite; a program needn't handle non-finite values.
Results may differ from the reference program's by a relative error of at most 0.024.
Values may be sent and summed in bfloat16 or wider, within the bound.
A program may use at most 320 MiB of HBM per device.

```python
import math
import jax
import jax.numpy as jnp
import numpy as np
from jax import lax

HEADS = 32
HEAD_DIM = 128
KV_HEADS = 4
REACH = 1
TOK_DEV = 128
D = 4096
KV_WIDTH = 1024
TOKENS = 1024
DOCS = 16
N_SECTION = 4
N_SEQ = 8


def block_scale(own_key, shape, pieces, smallest, high):
    def one(axis_at, blocks):
        steps = jax.random.uniform(jax.random.fold_in(jax.random.fold_in(own_key, 6), axis_at), (blocks,), jnp.float32, smallest / len(pieces), high / len(pieces))
        return jnp.repeat(jnp.exp(steps), shape[axis_at] // blocks).reshape((-1,) + (1,) * (len(shape) - axis_at - 1))

    level = one(*pieces[0])
    for cut in pieces[1:]:
        level = level * one(*cut)
    return level


def profile(count, total, reach, lean):
    portions = [(1 << 20) // math.isqrt(grade ** lean) + 1 for grade in range(2, count + 1)]
    rest, given = total - reach - (count - 1), [1] * (count - 1)
    while rest > 0:
        candidates = [i for i in range(count - 1) if given[i] < reach]
        whole, left = sum([portions[i] for i in candidates]), rest
        for i in candidates:
            addition = min(reach - given[i], max(1, left * portions[i] // whole), rest)
            given[i] = given[i] + addition
            rest = rest - addition
    return np.array([reach] + given)


def uneven(stream_key, count, total, bound, slope):
    if count == 2:
        one = jax.random.randint(stream_key, (), max(1, total - bound), min(bound, total - 1) + 1)
        return jnp.stack([one, total - one])
    tallies = jnp.asarray(profile(count, total, bound, slope), jnp.int32)
    twos = (count - 1) // 2
    donor, taker = tallies[1:1 + 2 * twos:2], tallies[2:2 + 2 * twos:2]
    slack = jnp.minimum(donor - 1, bound - taker)
    moved = jax.random.randint(jax.random.fold_in(stream_key, 1), (twos,), 0, 1 << 20) % (slack + 1)
    tallies = tallies.at[1:1 + 2 * twos:2].set(donor - moved).at[2:2 + 2 * twos:2].set(taker + moved)
    return tallies[jax.random.permutation(jax.random.fold_in(stream_key, 2), count)]


def bell_draw(own_key, extent, spread, most, cuts=(), held_as=jnp.bfloat16):
    result = jax.random.normal(own_key, extent, jnp.float32) * spread
    if len(cuts) > 0:
        result = block_scale(own_key, extent, cuts, -0.22, 0.18) * result
    return jnp.clip(result, min=-most, max=most).astype(held_as)


def setup_inputs(seed: int = 0) -> dict:
    key_of = jax.random.split(jax.random.key(seed), 8)
    x_a = bell_draw(key_of[0], (TOKENS, D), 1.0, 6.0, ((0, 8),))
    x_b = bell_draw(key_of[1], (TOKENS, D), 1.0, 6.0, ((0, 8),))
    grad_a = bell_draw(key_of[2], (TOKENS, D), 1.0, 6.0, ((0, 8),))
    grad_b = bell_draw(key_of[3], (TOKENS, D), 1.0, 6.0, ((0, 8),))
    gains = jnp.clip(1.0 + 0.1 * jax.random.normal(key_of[4], (N_SECTION, 2, D), jnp.float32), 0.5, 1.5)
    kv_weights = bell_draw(key_of[5], (N_SECTION, 2, D, KV_WIDTH), D ** -0.5, 0.09375, ((0, 4),))
    doc_lengths = jax.vmap(lambda own: uneven(own, DOCS, TOKENS, REACH * TOK_DEV, 1))(jax.random.split(key_of[6], 2)).reshape((2, DOCS)).astype(jnp.int32)
    return {"x_a": x_a, "x_b": x_b, "grad_a": grad_a, "grad_b": grad_b, "gains": gains, "kv_weights": kv_weights, "doc_lengths": doc_lengths}


epsilon = 1e-05

def normalize(stream, gain_row):
    widened = stream.astype(jnp.float32)
    square_mean = lax.optimization_barrier(jnp.mean(widened * widened, axis=-1, keepdims=True))
    return (widened * lax.rsqrt(square_mean + epsilon) * gain_row).astype(jnp.bfloat16)

def project_kv(stream, gain_row, weight_mat):
    return jnp.dot(normalize(stream, gain_row), weight_mat, preferred_element_type=jnp.float32).astype(jnp.bfloat16)

def doc_index(ends_row, places):
    return lax.optimization_barrier(jnp.sum((ends_row[None, :] <= places[:, None]).astype(jnp.int32), axis=1)).astype(jnp.int32)

def mix(stream, gain_row, pair_rows, docs_query, place_query, docs_key, place_key):
    row_count = stream.shape[0]
    widened = stream.astype(jnp.float32)
    normed = normalize(stream, gain_row)
    group_size = HEADS // KV_HEADS
    queries = normed.reshape(row_count, KV_HEADS, group_size, HEAD_DIM).astype(jnp.float32)
    key_count = pair_rows.shape[0]
    key_heads = pair_rows[:, :KV_HEADS * HEAD_DIM].reshape(key_count, KV_HEADS, HEAD_DIM).astype(jnp.float32)
    value_heads = pair_rows[:, KV_HEADS * HEAD_DIM:].reshape(key_count, KV_HEADS, HEAD_DIM).astype(jnp.float32)
    scores = jnp.einsum('tkgd,skd->kgts', queries, key_heads) * (1.0 / math.sqrt(HEAD_DIM))
    allowed = (docs_query[:, None] == docs_key[None, :]) & (place_key[None, :] <= place_query[:, None]) & (place_key[None, :] >= 0)
    scores = jnp.where(allowed, scores, -1e+30)
    largest = lax.optimization_barrier(jnp.max(scores, axis=-1, keepdims=True))
    powers = jnp.exp(scores - largest)
    weights = (powers / lax.optimization_barrier(jnp.sum(powers, axis=-1, keepdims=True))).astype(jnp.bfloat16)
    mixture = jnp.einsum('kgts,skd->tkgd', weights.astype(jnp.float32), value_heads)
    return (widened + mixture.reshape(row_count, HEADS * HEAD_DIM)).astype(jnp.bfloat16)

def whole_mix(stream, key_values, gain_row, ends_row):
    width = key_values.shape[-1]
    padded = jnp.concatenate([jnp.zeros((REACH * TOK_DEV, width), key_values.dtype), key_values], axis=0)

    def one_block(block):
        start = (block * TOK_DEV).astype(jnp.int32)
        rows = lax.dynamic_slice_in_dim(stream, start, TOK_DEV, 0)
        pairs = lax.dynamic_slice_in_dim(padded, start, (REACH + 1) * TOK_DEV, 0)
        query_places = (start + jnp.arange(TOK_DEV, dtype=jnp.int32)).astype(jnp.int32)
        key_places = (start - REACH * TOK_DEV + jnp.arange((REACH + 1) * TOK_DEV, dtype=jnp.int32)).astype(jnp.int32)
        return mix(rows, gain_row, pairs, doc_index(ends_row, query_places), query_places, doc_index(ends_row, key_places), key_places)
    outputs = lax.map(one_block, jnp.arange(N_SEQ, dtype=jnp.int32))
    return outputs.reshape(TOKENS, stream.shape[-1])

def reference(x_a, x_b, grad_a, grad_b, gains, kv_weights, doc_lengths):
    acts_all = []
    inputs_all = []
    pairs_all = []
    for direction in range(2):
        ends_row = jnp.cumsum(doc_lengths[direction]).astype(jnp.int32)
        stream = (x_a, x_b)[direction]
        cotangent = (grad_a, grad_b)[direction]
        owners = [layer_index if direction == 0 else N_SECTION - 1 - layer_index for layer_index in range(N_SECTION)]
        inputs_kept = []
        acts_by = [None] * N_SECTION
        ingrad_by = [None] * N_SECTION
        kvgrad_by = [None] * N_SECTION
        for layer_index in range(N_SECTION):
            owner_section = owners[layer_index]
            gain_row = gains[owner_section, direction]
            weight_mat = kv_weights[owner_section, direction]
            inputs_kept.append(stream)
            key_values = project_kv(stream, gain_row, weight_mat)
            stream = whole_mix(stream, key_values, gain_row, ends_row)
            acts_by[owner_section] = stream
        for layer_index in reversed(range(N_SECTION)):
            owner_section = owners[layer_index]
            gain_row = gains[owner_section, direction]
            weight_mat = kv_weights[owner_section, direction]
            layer_input = inputs_kept[layer_index]
            key_values = project_kv(layer_input, gain_row, weight_mat)
            _, pull_mix = jax.vjp(lambda stream_arg, pairs_arg: whole_mix(stream_arg, pairs_arg, gain_row, ends_row), layer_input, key_values)
            grad_stream, grad_pairs = pull_mix(cotangent)
            _, pull_proj = jax.vjp(lambda stream_arg: project_kv(stream_arg, gain_row, weight_mat), layer_input)
            cotangent = grad_stream + pull_proj(grad_pairs)[0]
            ingrad_by[owner_section] = cotangent
            kvgrad_by[owner_section] = grad_pairs
        acts_all.append(jnp.stack(acts_by))
        inputs_all.append(jnp.stack(ingrad_by))
        pairs_all.append(jnp.stack(kvgrad_by))
    return (jnp.stack(acts_all), jnp.stack(inputs_all), jnp.stack(pairs_all))
```

```python
import functools
import math

import jax
import jax.numpy as jnp
from jax import lax
from jax.experimental import pallas as pl
from jax.experimental.pallas import tpu as pltpu
from jax.sharding import PartitionSpec as P

HEADS = 32
HEAD_DIM = 128
KV_HEADS = 4
REACH = 1
GROUP = HEADS // KV_HEADS
SCALE = 1.0 / math.sqrt(HEAD_DIM)

epsilon = 1e-05

F32 = jnp.float32
BF16 = jnp.bfloat16


def passed_along(block, axis, distance):
    devices = range(lax.axis_size(axis))
    route = [(i - distance, i) for i in devices if i - distance in devices]
    return lax.ppermute(block, axis, route)


def dot(a, b, dims):
    return lax.dot_general(a, b, (dims, ((), ())), preferred_element_type=F32)


def project_kernel(slot_ref, h_ref, gain_ref, weight_ref, pairs_ref, normed_ref):
    @pl.when(pl.program_id(0) == 0)
    def _():
        widened = h_ref[...].astype(F32)
        square_mean = jnp.mean(widened * widened, axis=-1, keepdims=True)
        normed_ref[...] = (widened * lax.rsqrt(square_mean + epsilon) * gain_ref[0]).astype(BF16)

    pairs_ref[...] = dot(normed_ref[...], weight_ref[0], ((1,), (0,))).astype(BF16)


def project(slot, stream, gains, weights):
    rows, width = stream.shape
    pair_width = weights.shape[-1]
    tile = pair_width // 4
    return pl.pallas_call(
        project_kernel,
        grid_spec=pltpu.PrefetchScalarGridSpec(
            num_scalar_prefetch=1,
            grid=(pair_width // tile,),
            in_specs=[
                pl.BlockSpec((rows, width), lambda j, s: (0, 0)),
                pl.BlockSpec((1, 1, width), lambda j, s: (s[0], 0, 0)),
                pl.BlockSpec((1, width, tile), lambda j, s: (s[0], 0, j)),
            ],
            out_specs=[
                pl.BlockSpec((rows, tile), lambda j, s: (0, j)),
                pl.BlockSpec((rows, width), lambda j, s: (0, 0)),
            ],
        ),
        out_shape=[
            jax.ShapeDtypeStruct((rows, pair_width), BF16),
            jax.ShapeDtypeStruct((rows, width), BF16),
        ],
        cost_estimate=pl.CostEstimate(
            flops=2 * rows * width * pair_width,
            bytes_accessed=2 * width * pair_width,
            transcendentals=0,
        ),
        name="project",
    )(slot, stream, gains, weights)


def softmax_parts(query, keys, mask):
    scores = dot(query, keys, ((1,), (1,))) * SCALE
    scores = jnp.where(mask, scores, -1e30)
    powers = jnp.exp(scores - jnp.max(scores, axis=-1, keepdims=True))
    return powers * (1.0 / jnp.sum(powers, axis=-1, keepdims=True))


def mix_kernel(h_ref, normed_ref, kp_ref, ko_ref, vp_ref, vo_ref, mask_ref, out_ref):
    keys = jnp.concatenate([kp_ref[...], ko_ref[...]], axis=0)
    values = jnp.concatenate([vp_ref[...], vo_ref[...]], axis=0)
    mask = mask_ref[...] > 0.0
    for head in range(GROUP):
        cols = slice(head * HEAD_DIM, (head + 1) * HEAD_DIM)
        weights = softmax_parts(normed_ref[:, cols], keys, mask).astype(BF16)
        mixture = dot(weights, values, ((1,), (0,)))
        out_ref[:, cols] = (h_ref[:, cols].astype(F32) + mixture).astype(BF16)


def head_specs(rows):
    return [
        pl.BlockSpec((rows, HEAD_DIM), lambda k: (0, k)),
        pl.BlockSpec((rows, HEAD_DIM), lambda k: (0, k)),
        pl.BlockSpec((rows, HEAD_DIM), lambda k: (0, KV_HEADS + k)),
        pl.BlockSpec((rows, HEAD_DIM), lambda k: (0, KV_HEADS + k)),
    ]


def mix(stream, normed, earlier, own, mask):
    rows, width = stream.shape
    block = pl.BlockSpec((rows, GROUP * HEAD_DIM), lambda k: (0, k))
    return pl.pallas_call(
        mix_kernel,
        grid=(KV_HEADS,),
        in_specs=[block, block] + head_specs(rows) + [pl.BlockSpec(mask.shape, lambda k: (0, 0))],
        out_specs=block,
        out_shape=jax.ShapeDtypeStruct((rows, width), BF16),
        cost_estimate=pl.CostEstimate(
            flops=8 * rows * rows * width, bytes_accessed=6 * rows * width, transcendentals=0
        ),
        name="mix",
    )(stream, normed, earlier, own, earlier, own, mask)


def reverse_kernel(
    c_ref, normed_ref, kp_ref, ko_ref, vp_ref, vo_ref, mask_ref,
    dq_ref, dkp_ref, dko_ref, dvp_ref, dvo_ref,
):
    rows = c_ref.shape[0]
    keys = jnp.concatenate([kp_ref[...], ko_ref[...]], axis=0)
    values = jnp.concatenate([vp_ref[...], vo_ref[...]], axis=0)
    mask = mask_ref[...] > 0.0
    weight_list, score_list, query_list, cot_list = [], [], [], []
    for head in range(GROUP):
        cols = slice(head * HEAD_DIM, (head + 1) * HEAD_DIM)
        query = normed_ref[:, cols]
        cot = c_ref[:, cols]
        weights = softmax_parts(query, keys, mask)
        grad_w = dot(cot, values, ((1,), (1,)))
        inner = jnp.sum(grad_w * weights, axis=-1, keepdims=True)
        grad_s = (weights * (grad_w - inner) * SCALE).astype(BF16)
        dq_ref[:, cols] = dot(grad_s, keys, ((1,), (0,))).astype(BF16)
        weight_list.append(weights.astype(BF16))
        score_list.append(grad_s)
        query_list.append(query)
        cot_list.append(cot)
    all_s = jnp.concatenate(score_list, axis=0)
    all_w = jnp.concatenate(weight_list, axis=0)
    all_q = jnp.concatenate(query_list, axis=0)
    all_c = jnp.concatenate(cot_list, axis=0)
    grad_k = dot(all_s, all_q, ((0,), (0,))).astype(BF16)
    grad_v = dot(all_w, all_c, ((0,), (0,))).astype(BF16)
    dkp_ref[...] = grad_k[:rows]
    dko_ref[...] = grad_k[rows:]
    dvp_ref[...] = grad_v[:rows]
    dvo_ref[...] = grad_v[rows:]


def reverse_mix(cotangent, normed, earlier, own, mask):
    rows, width = cotangent.shape
    block = pl.BlockSpec((rows, GROUP * HEAD_DIM), lambda k: (0, k))
    half = pl.BlockSpec((rows, HEAD_DIM), lambda k: (0, k))
    half_shape = jax.ShapeDtypeStruct((rows, KV_HEADS * HEAD_DIM), BF16)
    return pl.pallas_call(
        reverse_kernel,
        grid=(KV_HEADS,),
        in_specs=[block, block] + head_specs(rows) + [pl.BlockSpec(mask.shape, lambda k: (0, 0))],
        out_specs=[block, half, half, half, half],
        out_shape=[jax.ShapeDtypeStruct((rows, width), BF16)] + [half_shape] * 4,
        cost_estimate=pl.CostEstimate(
            flops=20 * rows * rows * width, bytes_accessed=6 * rows * width, transcendentals=0
        ),
        name="reverse_mix",
    )(cotangent, normed, earlier, own, earlier, own, mask)


def reverse_project_kernel(
    steps, slot_ref, c_ref, dq_ref, h_ref, gain_ref, dk_ref, rk_ref, dv_ref, rv_ref, weight_ref,
    total_ref, pairs_ref, grad_scr,
):
    step = pl.program_id(0)
    tile = weight_ref.shape[1]

    @pl.when(step == 0)
    def _():
        half = dk_ref.shape[1]
        pairs_ref[:, :half] = (dk_ref[...].astype(F32) + rk_ref[...].astype(F32)).astype(BF16)
        pairs_ref[:, half:] = (dv_ref[...].astype(F32) + rv_ref[...].astype(F32)).astype(BF16)

    grad_scr[step] = dot(pairs_ref[...], weight_ref[0], ((1,), (1,))).astype(BF16)

    @pl.when(step == steps - 1)
    def _():
        widened = h_ref[...].astype(F32)
        width = widened.shape[1]
        rstd = lax.rsqrt(jnp.mean(widened * widened, axis=-1, keepdims=True) + epsilon)
        inner = jnp.zeros_like(rstd)
        for j in range(steps):
            cols = slice(j * tile, (j + 1) * tile)
            grad_n = (grad_scr[j].astype(F32) + dq_ref[:, cols].astype(F32)) * gain_ref[0, :, cols]
            inner = inner + jnp.sum(grad_n * widened[:, cols], axis=-1, keepdims=True)
        factor = inner * (1.0 / width) * rstd * rstd * rstd
        for j in range(steps):
            cols = slice(j * tile, (j + 1) * tile)
            grad_n = (grad_scr[j].astype(F32) + dq_ref[:, cols].astype(F32)) * gain_ref[0, :, cols]
            grad_h = grad_n * rstd - widened[:, cols] * factor
            total_ref[:, cols] = (c_ref[:, cols].astype(F32) + grad_h).astype(BF16)


def reverse_project(slot, cotangent, grad_q, stream, gains, grads, weights):
    rows, width = stream.shape
    pair_width = weights.shape[-1]
    steps = 4
    tile = width // steps
    full = pl.BlockSpec((rows, width), lambda j, s: (0, 0))
    half = pl.BlockSpec((rows, pair_width // 2), lambda j, s: (0, 0))
    return pl.pallas_call(
        functools.partial(reverse_project_kernel, steps),
        grid_spec=pltpu.PrefetchScalarGridSpec(
            num_scalar_prefetch=1,
            grid=(steps,),
            in_specs=[full, full, full, pl.BlockSpec((1, 1, width), lambda j, s: (s[0], 0, 0))]
            + [half] * 4
            + [pl.BlockSpec((1, tile, pair_width), lambda j, s: (s[0], j, 0))],
            out_specs=[full, pl.BlockSpec((rows, pair_width), lambda j, s: (0, 0))],
            scratch_shapes=[pltpu.VMEM((steps, rows, tile), BF16)],
        ),
        out_shape=[
            jax.ShapeDtypeStruct((rows, width), BF16),
            jax.ShapeDtypeStruct((rows, pair_width), BF16),
        ],
        cost_estimate=pl.CostEstimate(
            flops=2 * rows * width * pair_width,
            bytes_accessed=2 * width * pair_width,
            transcendentals=0,
        ),
        name="reverse_project",
    )(slot, cotangent, grad_q, stream, gains, *grads, weights)


def per_device(x_a, x_b, grad_a, grad_b, gains, kv_weights, doc_lengths):
    count = lax.axis_size("section")
    section = lax.axis_index("section")
    shard = lax.axis_index("seq")
    rows = x_a.shape[0]
    places = shard * rows + jnp.arange(rows, dtype=jnp.int32)
    key_places = (shard - REACH) * rows + jnp.arange((REACH + 1) * rows, dtype=jnp.int32)
    ends = jnp.cumsum(doc_lengths, axis=1)

    def mask_of(direction):
        docs_q = jnp.sum((ends[direction][None, :] <= places[:, None]).astype(jnp.int32), axis=1)
        docs_k = jnp.sum((ends[direction][None, :] <= key_places[:, None]).astype(jnp.int32), axis=1)
        allowed = (
            (docs_q[:, None] == docs_k[None, :])
            & (key_places[None, :] <= places[:, None])
            & (key_places[None, :] >= 0)
        )
        return allowed.astype(F32)

    mask_down, mask_up = mask_of(0), mask_of(1)
    gain_pair = gains[0][:, None, :]
    weight_pair = kv_weights[0]

    saved = {}
    held_down, held_up = x_a, x_b
    for step in range(count):
        down = section == step
        up = section == count - 1 - step
        slot = jnp.where(down, 0, 1).astype(jnp.int32)[None]
        stream = jnp.where(down, held_down, held_up)
        mask = jnp.where(down, mask_down, mask_up)
        own, normed = project(slot, stream, gain_pair, weight_pair)
        earlier = passed_along(own, "seq", REACH)
        output = mix(stream, normed, earlier, own, mask)
        if step + 1 < count:
            held_down = passed_along(output, "section", 1)
            held_up = passed_along(output, "section", -1)
        fresh = (stream, normed, own, earlier, output)
        for name, chosen in (("down", down), ("up", up)):
            before = saved.get(name)
            saved[name] = (
                fresh
                if before is None
                else tuple(jnp.where(chosen, new, old) for new, old in zip(fresh, before))
            )
    acts_out = jnp.stack([saved["down"][4], saved["up"][4]])[:, None]

    held_down, held_up = grad_a, grad_b
    results = {}
    for step in range(count):
        down = section == count - 1 - step
        up = section == step
        slot = jnp.where(down, 0, 1).astype(jnp.int32)[None]
        cotangent = jnp.where(down, held_down, held_up)
        stream, normed, own, earlier = (
            jnp.where(down, a, b) for a, b in zip(saved["down"][:4], saved["up"][:4])
        )
        mask = jnp.where(down, mask_down, mask_up)
        grad_q, dkp, dko, dvp, dvo = reverse_mix(cotangent, normed, earlier, own, mask)
        rk = passed_along(dkp, "seq", 0 - REACH)
        rv = passed_along(dvp, "seq", 0 - REACH)
        total, pairs = reverse_project(
            slot, cotangent, grad_q, stream, gain_pair, (dko, rk, dvo, rv), weight_pair
        )
        if step + 1 < count:
            held_down = passed_along(total, "section", -1)
            held_up = passed_along(total, "section", 1)
        fresh = (total, pairs)
        for name, chosen in (("down", down), ("up", up)):
            before = results.get(name)
            results[name] = (
                fresh
                if before is None
                else tuple(jnp.where(chosen, new, old) for new, old in zip(fresh, before))
            )
    ingrad_out = jnp.stack([results["down"][0], results["up"][0]])[:, None]
    kvgrad_out = jnp.stack([results["down"][1], results["up"][1]])[:, None]
    return (acts_out, ingrad_out, kvgrad_out)


def solution(mesh):
    in_specs = (
        P("seq", None),
        P("seq", None),
        P("seq", None),
        P("seq", None),
        P("section", None, None),
        P("section", None, None, None),
        P(),
    )
    out_specs = (
        P(None, "section", "seq", None),
        P(None, "section", "seq", None),
        P(None, "section", "seq", None),
    )
    return jax.shard_map(
        per_device, mesh=mesh, in_specs=in_specs, out_specs=out_specs, check_vma=False
    )
```
